256 devices in a mesh: dp: 16 (over z, core), ctx: 16 (over y, x).
Axes of the slice: x: 4, y: 4, z: 8, core: 2. Of those that a mesh axis runs over, the one named last changes fastest.
Arguments:
- queries: bfloat16 [16, 2048, 4096], P('dp', 'ctx'), may hold values from -48 to 48
- keys: bfloat16 [16, 2048, 512], P('dp', 'ctx'), may hold values from -14 to 14
- values: bfloat16 [16, 2048, 512], P('dp', 'ctx'), may hold values from -6 to 6
- out_grad: bfloat16 [16, 2048, 4096], P('dp', 'ctx'), may hold values from -0.5 to 0.5
- doc_blocks: int32 [16, 3], P('dp'), may hold values from 1 to 8, 16 in all within a row
- doc_temp: int32 [16, 3], P('dp'), may hold values from 0 to 3
- temp_table: float32 [4], replicated, may hold values from 0.1 to 0.3
- dest: int32 [16, 16, 1], P('dp'), may hold values from 0 to 15; in each aligned block of 16 rows (0 to 15, 16 to 31, ..., all dimensions but the last counted through in order) at most 3 rows name the same one
Outputs:
- dq_rows: bfloat16 [16, 6144, 4096], P('dp', 'ctx')
- dkv_rows: bfloat16 [16, 6144, 1024], P('dp', 'ctx')
- temp_grad: float32 [4], replicated
The draws below stay inside these ranges and needn't reach their ends.
Inputs may be any that keep to these rules, and one draw needn't show every extreme that they name: `doc_blocks`: the documents of a sequence follow one another from its first block and fill its 16 blocks exactly; the longest has 8 blocks. `dest`: at most 3 blocks of one sequence go to one loader shard, and some shard receives exactly 3 blocks of some sequence.
All inputs are finite; a program needn't handle non-finite values.
Results may differ from the reference program's by a relative error of at most 0.0051.
Values may be sent and summed in bfloat16 or wider, within the bound.
No kernel may reach another device: no remote copies, remote signals or barrier semaphores. Data moves between devices by JAX's collectives and lax.ppermute only.
A program may use at most 128 MiB of HBM per device.

```python
import math
import jax
import jax.numpy as jnp
import numpy as np
from jax import lax

HQ = 32
KV = 4
DH = 128
BLK = 128
CAP = 3
DOCS = 3
TEMPS = 4
BATCH = 16
SEQ = 2048
NBLK = 16
MOSTB = 8
N_CTX = 16


def paired_draw(base_key):
    query_key = jax.random.fold_in(base_key, 101)
    keyvec_key = jax.random.fold_in(base_key, 102)
    key_field = jnp.clip(jax.random.normal(keyvec_key, (BATCH, SEQ, KV, DH), jnp.float32), -4.0, 4.0)
    query_field = jnp.clip(jax.random.normal(query_key, (BATCH, SEQ, HQ, DH), jnp.float32), -4.0, 4.0)
    return (query_field.reshape(BATCH, SEQ, HQ * DH), key_field.reshape(BATCH, SEQ, KV * DH))


def draw_queries(key, part):
    return paired_draw(key)[0].astype(jnp.bfloat16)


def draw_keys(key, part):
    return paired_draw(key)[1].astype(jnp.bfloat16)


def place_ends(entries, key, least, largest):
    longest = entries.shape.index(max(entries.shape))
    spots = []
    for shift in (0, 1):
        where = [jax.random.randint(jax.random.fold_in(key, axis), (), 0, length) for axis, length in enumerate(entries.shape)]
        where[longest] = (where[longest] + shift) % entries.shape[longest]
        spots.append(tuple(where))
    return entries.at[spots[0]].set(least).at[spots[1]].set(largest)


def block_levels(key, dims, shards, low, top_value):
    factor_of, own = 1.0, jax.random.fold_in(key, 6)
    for dim, shards_of in shards:
        steps = jnp.exp(jax.random.uniform(jax.random.fold_in(own, dim), (shards_of,), jnp.float32, low / len(shards), top_value / len(shards)))
        factor_of = factor_of * jnp.repeat(steps, dims[dim] // shards_of).reshape([-1 if axis == dim else 1 for axis in range(len(dims))])
    return factor_of


def split_up(count, total, limit, slope):
    weights = [(1 << 20) // math.isqrt(grade ** slope) + 1 for grade in range(2, count + 1)]
    surplus, given = total - limit - (count - 1), [1] * (count - 1)
    while surplus > 0:
        movable = [i for i in range(count - 1) if given[i] < limit]
        mass, remaining = sum([weights[i] for i in movable]), surplus
        for i in movable:
            addition = min(limit - given[i], max(1, remaining * weights[i] // mass), surplus)
            given[i] = given[i] + addition
            surplus = surplus - addition
    return np.array([limit] + given)


def ragged_sizes(key, count, total, bound, lean):
    if count == 2:
        one = jax.random.randint(key, (), max(1, total - bound), min(bound, total - 1) + 1)
        return jnp.stack([one, total - one])
    sizes = jnp.asarray(split_up(count, total, bound, lean), jnp.int32)
    twos = (count - 1) // 2
    source_of, sink = sizes[1:1 + 2 * twos:2], sizes[2:2 + 2 * twos:2]
    margin = jnp.minimum(source_of - 1, bound - sink)
    passed = jax.random.randint(jax.random.fold_in(key, 1), (twos,), 0, 1 << 20) % (margin + 1)
    sizes = sizes.at[1:1 + 2 * twos:2].set(source_of - passed).at[2:2 + 2 * twos:2].set(sink + passed)
    return sizes[jax.random.permutation(jax.random.fold_in(key, 2), count)]


def deal_out(own_key, own, number, rows, number_of, top, limit, skew):
    order = jax.random.permutation(own_key, number_of)
    packed, common = portions_of(number_of, rows * top, limit, skew, True), portions_of(number_of, rows * top, limit, skew, False)
    places = jnp.arange(number_of)

    def named(tallies, rotation):
        used = int((tallies > 0).sum())
        fixed = max(1, used // 4)
        moved = fixed + (places - fixed + rotation * (used - fixed)) % max(1, number_of - fixed)
        return jnp.zeros((number_of,), jnp.int32).at[order[jnp.where(places < fixed, places, moved)]].set(jnp.asarray(tallies, jnp.int32))

    tallies = jnp.where(number % 4 == 0, named(packed, number // 4), named(common, number - number // 4 - 1))
    mixed = jax.random.permutation(jax.random.fold_in(own, 3), number_of)
    giver, receiver = mixed[0:number_of // 2 * 2:2], mixed[1:number_of // 2 * 2:2]
    room = jnp.minimum(tallies[giver] - 1, limit - tallies[receiver]) // 2
    room = jnp.where((giver == order[0]) | (receiver == order[0]) | (tallies[receiver] == 0), 0, jnp.maximum(room, 0))
    moved = jax.random.randint(jax.random.fold_in(own, 4), (number_of // 2,), 0, 1 << 20) % (room + 1)
    tallies = tallies.at[giver].add(-moved).at[receiver].add(moved)
    members = jnp.searchsorted(jnp.cumsum(tallies), jnp.arange(rows * top), side="right").astype(jnp.int32)
    table = members.reshape(top, rows).T
    table = table[jax.random.permutation(jax.random.fold_in(own, 1), rows)]
    rotation = jax.random.randint(jax.random.fold_in(own, 2), (rows, 1), 0, top)
    return jnp.take_along_axis(table, (jnp.arange(top)[None, :] + rotation) % top, axis=1)


def portions_of(number_of, total, bound, lean, full):
    portions = [(1 << 20) // math.isqrt(standing ** lean) + 1 for standing in range(1, number_of + 1)]
    largest = bound if full else min(bound, max(-(-total // number_of), total * portions[0] // sum(portions)))
    least = 1 if total - largest >= number_of - 1 else 0
    given, surplus = [largest] + [least] * (number_of - 1), total - largest - least * (number_of - 1)
    while surplus > 0:
        free = [i for i in range(1, number_of) if given[i] < largest] or [i for i in range(1, number_of) if given[i] < bound]
        pool, remaining = sum([portions[i] for i in free]), surplus
        for i in free:
            more = min(bound - given[i], max(1, remaining * portions[i] // pool), surplus)
            given[i] = given[i] + more
            surplus = surplus - more
    return np.array(given)


def scatter_about(own_key, extent, deviation, bound, shards=(), held_as=jnp.bfloat16):
    loudness = block_levels(own_key, extent, shards, -0.22, 0.18) if shards else 1.0
    values = jax.random.normal(own_key, extent, jnp.float32) * deviation * loudness
    return jnp.minimum(jnp.maximum(values, -bound), bound).astype(held_as)


def setup_inputs(seed: int = 0) -> dict:
    arg_keys = jax.random.split(jax.random.key(seed), 9)
    queries = draw_queries(jax.random.fold_in(arg_keys[8], 71), 0)
    keys = draw_keys(jax.random.fold_in(arg_keys[8], 71), 0)
    values = scatter_about(arg_keys[2], (BATCH, SEQ, KV * DH), 1.0, 6.0, ((0, 16), (1, 16)))
    out_grad = scatter_about(arg_keys[3], (BATCH, SEQ, HQ * DH), (DH ** -0.5), 0.5, ((0, 16), (1, 16)))
    doc_blocks = jax.vmap(lambda own: ragged_sizes(own, DOCS, NBLK, MOSTB, 1))(jax.random.split(arg_keys[4], BATCH)).reshape((BATCH, DOCS)).astype(jnp.int32)
    doc_temp = place_ends(jax.random.randint(arg_keys[5], (BATCH, DOCS), 0, TEMPS), jax.random.fold_in(arg_keys[5], 1), 0, TEMPS - 1).astype(jnp.int32)
    temp_table = jnp.clip(jnp.exp(jax.random.uniform(arg_keys[6], (TEMPS,), jnp.float32, math.log(0.1), math.log(0.3))), 0.1, 0.3)
    dest_keys = jax.random.split(jax.random.fold_in(arg_keys[7], 1), BATCH * NBLK // NBLK)
    dest_turns = jax.random.permutation(jax.random.fold_in(arg_keys[7], 3), BATCH * NBLK // NBLK)
    dest = jax.vmap(lambda own, number: deal_out(jax.random.fold_in(arg_keys[7], 2), own, number, NBLK, N_CTX, 1, CAP, 1))(dest_keys, dest_turns).reshape((BATCH, NBLK, 1))
    return dict(queries=queries, keys=keys, values=values, out_grad=out_grad, doc_blocks=doc_blocks, doc_temp=doc_temp, temp_table=temp_table, dest=dest)


def sequence_grads(queries_seq, keys_seq, values_seq, grad_seq, doc_len, doc_temp_seq, targets, temp_table):
    group_size = HQ // KV
    positions = jnp.arange(SEQ, dtype=jnp.int32)
    doc_ends = jnp.cumsum(doc_len).astype(jnp.int32) * BLK
    doc_of = lax.optimization_barrier(jnp.sum((positions[:, None] >= doc_ends[None, :]).astype(jnp.int32), axis=1))
    doc_onehot = (doc_of[:, None] == jnp.arange(DOCS, dtype=jnp.int32)[None, :]).astype(jnp.float32)
    temp_onehot = (doc_temp_seq[:, None] == jnp.arange(TEMPS, dtype=jnp.int32)[None, :]).astype(jnp.float32)
    temp_doc = lax.optimization_barrier(jnp.sum(temp_onehot * temp_table[None, :], axis=1))
    log_len = jnp.log((doc_len * BLK).astype(jnp.float32)) / math.sqrt(DH)
    scale_tok = lax.optimization_barrier(jnp.sum(doc_onehot * (temp_doc * log_len)[None, :], axis=1))
    allowed = (doc_of[:, None] == doc_of[None, :]) & (positions[None, :] <= positions[:, None])
    q_heads = queries_seq.reshape(SEQ, HQ, DH)
    g_heads = grad_seq.reshape(SEQ, HQ, DH)
    k_heads = keys_seq.reshape(SEQ, KV, DH)
    v_heads = values_seq.reshape(SEQ, KV, DH)

    def one_head(head_index):
        q_one = lax.dynamic_index_in_dim(q_heads, head_index, 1, keepdims=False)
        g_one = lax.dynamic_index_in_dim(g_heads, head_index, 1, keepdims=False)
        k_one = lax.dynamic_index_in_dim(k_heads, head_index // group_size, 1, keepdims=False)
        v_one = lax.dynamic_index_in_dim(v_heads, head_index // group_size, 1, keepdims=False)
        scores = jnp.dot(q_one, k_one.T, preferred_element_type=jnp.float32)
        logits = jnp.where(allowed, scale_tok[:, None] * scores, -jnp.inf)
        row_max = lax.optimization_barrier(jnp.max(logits, axis=1, keepdims=True))
        expon = jnp.exp(logits - row_max)
        probs = expon / lax.optimization_barrier(jnp.sum(expon, axis=1, keepdims=True))
        dprob = jnp.dot(g_one, v_one.T, preferred_element_type=jnp.float32)
        dlogit = probs * (dprob - lax.optimization_barrier(jnp.sum(probs * dprob, axis=1, keepdims=True)))
        scaled = (scale_tok[:, None] * dlogit).astype(jnp.bfloat16)
        probs_bf = probs.astype(jnp.bfloat16)
        dq_one = jnp.dot(scaled, k_one, preferred_element_type=jnp.float32)
        dk_one = jnp.dot(scaled.T, q_one, preferred_element_type=jnp.float32)
        dv_one = jnp.dot(probs_bf.T, g_one, preferred_element_type=jnp.float32)
        terms = lax.optimization_barrier(jnp.sum(dlogit * scores, axis=1))
        return (dq_one, dk_one, dv_one, terms)
    dq_all, dk_all, dv_all, head_terms = lax.map(one_head, jnp.arange(HQ, dtype=jnp.int32))
    dq_tok = jnp.transpose(dq_all, (1, 0, 2)).reshape(SEQ, HQ * DH).astype(jnp.bfloat16)
    dk_tok = jnp.transpose(lax.optimization_barrier(jnp.sum(dk_all.reshape(KV, group_size, SEQ, DH), axis=1)), (1, 0, 2)).reshape(SEQ, KV * DH)
    dv_tok = jnp.transpose(lax.optimization_barrier(jnp.sum(dv_all.reshape(KV, group_size, SEQ, DH), axis=1)), (1, 0, 2)).reshape(SEQ, KV * DH)
    dkv_tok = jnp.concatenate([dk_tok, dv_tok], axis=1).astype(jnp.bfloat16)
    token_terms = lax.optimization_barrier(jnp.sum(head_terms, axis=0))
    doc_terms = lax.optimization_barrier(jnp.sum(doc_onehot * token_terms[:, None], axis=0)) * log_len
    temp_part = lax.optimization_barrier(jnp.sum(temp_onehot * doc_terms[:, None], axis=0))
    matches = (targets[:, None] == jnp.arange(N_CTX, dtype=jnp.int32)[None, :]).astype(jnp.int32)
    earlier = jnp.cumsum(matches, axis=0) - matches
    ranking = lax.optimization_barrier(jnp.sum(earlier * matches, axis=1)).astype(jnp.int32)
    slot_ids = (targets * CAP + ranking).astype(jnp.int32)
    dq_blocks = dq_tok.reshape(NBLK, BLK, HQ * DH)
    dkv_blocks = dkv_tok.reshape(NBLK, BLK, 2 * KV * DH)
    dq_slots = jnp.zeros((N_CTX * CAP, BLK, HQ * DH), jnp.bfloat16).at[slot_ids].set(dq_blocks)
    dkv_slots = jnp.zeros((N_CTX * CAP, BLK, 2 * KV * DH), jnp.bfloat16).at[slot_ids].set(dkv_blocks)
    return (dq_slots.reshape(N_CTX * CAP * BLK, HQ * DH), dkv_slots.reshape(N_CTX * CAP * BLK, 2 * KV * DH), temp_part)

def reference(queries, keys, values, out_grad, doc_blocks, doc_temp, temp_table, dest):

    def per_sequence(items):
        return sequence_grads(items[0], items[1], items[2], items[3], items[4], items[5], items[6], temp_table)
    dq_rows, dkv_rows, temp_parts = lax.map(per_sequence, (queries, keys, values, out_grad, doc_blocks, doc_temp, dest[:, :, 0]))
    return (dq_rows, dkv_rows, lax.optimization_barrier(jnp.sum(temp_parts, axis=0)))
```

```python
import functools
import math

import jax
import jax.numpy as jnp
from jax import lax
from jax.experimental import pallas as pl
from jax.experimental.pallas import tpu as pltpu
from jax.sharding import PartitionSpec as P

KV = 4
DH = 128
BLK = 128
CAP = 3
NBLK = 16
DOCS = 3
TEMPS = 4
MOSTB = 8
NCTX = 16
GRP = 4
QR = BLK // GRP
ROUTE = CAP * QR
PAY = ROUTE + 16
LOG_LEN = [math.log(BLK * n) / math.sqrt(DH) for n in range(1, MOSTB + 1)]
LOG2E = math.log2(math.e)
GROUPS = [[GRP * y + x for x in range(GRP)] for y in range(NCTX // GRP)]
VMEM = pl.BlockSpec(memory_space=pltpu.VMEM)
SMEM = pl.BlockSpec(memory_space=pltpu.SMEM)


def pack_kernel(q_ref, g_ref, k_ref, v_ref, out_ref):
    for j in range(NCTX):
        kv = j // GRP
        out_ref[j, :, 0:256] = q_ref[0, :, j * 256 : (j + 1) * 256]
        out_ref[j, :, 256:512] = g_ref[0, :, j * 256 : (j + 1) * 256]
        out_ref[j, :, 512:640] = k_ref[0, :, kv * DH : (kv + 1) * DH]
        out_ref[j, :, 640:768] = v_ref[0, :, kv * DH : (kv + 1) * DH]


def pick(index, entries):
    value = entries[0]
    for place in range(1, len(entries)):
        value = jnp.where(index == place, entries[place], value)
    return value


def attention_kernel(len_ref, temp_ref, table_ref, dest_ref, x_ref, dq_ref, dkv_ref, temp_out_ref,
                     kt_ref, acc_ref, term_ref, count_ref):
    lens = [len_ref[0, d] for d in range(DOCS)]
    ends = [lens[0], lens[0] + lens[1]]
    dq_ref[...] = jnp.zeros_like(dq_ref)
    acc_ref[...] = jnp.zeros_like(acc_ref)
    term_ref[...] = jnp.zeros_like(term_ref)
    for s in range(NCTX):
        count_ref[s] = 0
    for b in range(NBLK):
        kt_ref[:, b * BLK : (b + 1) * BLK] = (
            x_ref[b, :, 512:640].astype(jnp.float32).T.astype(jnp.bfloat16)
        )

    def block_step(b, carry):
        doc = (b >= ends[0]).astype(jnp.int32) + (b >= ends[1]).astype(jnp.int32)
        start = pick(doc, [0, ends[0], ends[1]])
        width = b - start + 1
        scale = table_ref[temp_ref[0, doc]] * pick(pick(doc, lens) - 1, LOG_LEN)
        shard = dest_ref[0, b, 0]
        rank = count_ref[shard]
        count_ref[shard] = rank + 1
        slot = jnp.minimum(shard * CAP + rank, NCTX * CAP - 1)
        own = x_ref[b]
        q_two = jnp.concatenate([own[:, 0:128], own[:, 128:256]], axis=0)
        g_two = jnp.concatenate([own[:, 256:384], own[:, 384:512]], axis=0)

        def run(n):
            k_win = x_ref[pl.ds(start, n), :, 512:640].reshape(n * BLK, DH)
            v_win = x_ref[pl.ds(start, n), :, 640:768].reshape(n * BLK, DH)
            contract = (((1,), (1,)), ((), ()))
            raw = lax.dot_general(k_win, q_two, contract, preferred_element_type=jnp.float32)
            dprob = lax.dot_general(v_win, g_two, contract, preferred_element_type=jnp.float32)
            logit = raw * (scale * LOG2E)
            row = lax.broadcasted_iota(jnp.int32, (BLK, 2 * BLK), 0)
            col = lax.broadcasted_iota(jnp.int32, (BLK, 2 * BLK), 1) % BLK
            last = jnp.where(row <= col, logit[(n - 1) * BLK :], -jnp.inf)
            logit = last if n == 1 else jnp.concatenate([logit[: (n - 1) * BLK], last], axis=0)
            top = jnp.max(logit, axis=0, keepdims=True)
            expon = jnp.exp2(logit - top)
            inverse = 1.0 / jnp.sum(expon, axis=0, keepdims=True)
            probs = expon * inverse
            mean = jnp.sum(probs * dprob, axis=0, keepdims=True)
            dlogit = probs * (dprob - mean)
            term_ref[doc] += jnp.sum((dlogit * raw).reshape(-1, 8, 2 * BLK), axis=0)
            scaled = (dlogit * scale).astype(jnp.bfloat16)
            probs_bf = probs.astype(jnp.bfloat16)
            dk = jnp.dot(scaled, q_two, preferred_element_type=jnp.float32)
            dv = jnp.dot(probs_bf, g_two, preferred_element_type=jnp.float32)
            acc_ref[pl.ds(start, n), :, 0:128] += dk.reshape(n, BLK, DH)
            acc_ref[pl.ds(start, n), :, 128:256] += dv.reshape(n, BLK, DH)
            kt_win = kt_ref[:, pl.ds(pl.multiple_of(start * BLK, BLK), n * BLK)]
            dq_t = jnp.dot(kt_win, scaled, preferred_element_type=jnp.float32)
            dq_ref[slot, :, 0:128] = dq_t[:, 0:128].T.astype(jnp.bfloat16)
            dq_ref[slot, :, 128:256] = dq_t[:, 128:256].T.astype(jnp.bfloat16)

        for n in range(1, MOSTB + 1):
            pl.when(width == n)(functools.partial(run, n))
        return carry

    lax.fori_loop(0, NBLK, block_step, 0)
    for part in range(GRP):
        dkv_ref[part] = acc_ref[:, part * QR : (part + 1) * QR, :]
    lane = lax.broadcasted_iota(jnp.int32, (8, 128), 1)
    row = lax.broadcasted_iota(jnp.int32, (8, 128), 0)
    total = jnp.zeros((8, 128), jnp.float32)
    for d in range(DOCS):
        amount = jnp.sum(term_ref[d]) * pick(lens[d] - 1, LOG_LEN)
        total += jnp.where((lane == temp_ref[0, d]) & (row == 0), amount, 0.0)
    temp_out_ref[...] = total


def route_kernel(dest_ref, part_ref, temp_ref, out_ref, count_ref):
    out_ref[...] = jnp.zeros_like(out_ref)
    for s in range(NCTX):
        count_ref[s] = 0
    high = temp_ref[...].astype(jnp.bfloat16).astype(jnp.float32)
    rest = temp_ref[...] - high
    middle = rest.astype(jnp.bfloat16).astype(jnp.float32)
    low = rest - middle
    left = jnp.concatenate([high, middle], axis=0).astype(jnp.bfloat16)
    right = jnp.concatenate([low, jnp.zeros_like(low)], axis=0).astype(jnp.bfloat16)
    for s in range(NCTX):
        out_ref[s, ROUTE:PAY, 0:128] = left
        out_ref[s, ROUTE:PAY, 128:256] = right
    for b in range(NBLK):
        shard = dest_ref[0, b, 0]
        rank = count_ref[shard]
        count_ref[shard] = rank + 1
        row = pl.multiple_of(jnp.minimum(rank, CAP - 1) * QR, QR)
        out_ref[shard, pl.ds(row, QR), :] = part_ref[b].astype(jnp.bfloat16)


def dq_rows_kernel(in_ref, out_ref):
    for j in range(NCTX):
        out_ref[0, :, j * 256 : (j + 1) * 256] = in_ref[j]


def dkv_rows_kernel(in_ref, out_ref, temp_ref):
    total = jnp.zeros((8, 128), jnp.float32)
    for j in range(NCTX):
        kv, part = j // GRP, j % GRP
        for r in range(CAP):
            rows = pl.ds(r * BLK + part * QR, QR)
            out_ref[0, rows, kv * DH : (kv + 1) * DH] = in_ref[j, r * QR : (r + 1) * QR, 0:128]
            out_ref[0, rows, (KV + kv) * DH : (KV + kv + 1) * DH] = (
                in_ref[j, r * QR : (r + 1) * QR, 128:256]
            )
        left = in_ref[j, ROUTE:PAY, 0:128].astype(jnp.float32)
        right = in_ref[j, ROUTE:PAY, 128:256].astype(jnp.float32)
        total += (left[0:8] + left[8:16]) + right[0:8]
    temp_ref[...] = total


def shards(queries, keys, values, out_grad, doc_blocks, doc_temp, temp_table, dest):
    params = functools.partial(pltpu.CompilerParams, vmem_limit_bytes=40 * 1024 * 1024)
    send = pl.pallas_call(
        pack_kernel,
        out_shape=jax.ShapeDtypeStruct((NCTX, BLK, 768), jnp.bfloat16),
        in_specs=[VMEM] * 4,
        out_specs=VMEM,
        compiler_params=params(),
        name="pack",
    )(queries, out_grad, keys, values)
    recv = lax.all_to_all(send, "ctx", split_axis=0, concat_axis=0, tiled=True)
    dq_slots, dkv_part, temp_part = pl.pallas_call(
        attention_kernel,
        out_shape=(
            jax.ShapeDtypeStruct((NCTX * CAP, BLK, 256), jnp.bfloat16),
            jax.ShapeDtypeStruct((GRP, NBLK, QR, 256), jnp.float32),
            jax.ShapeDtypeStruct((8, 128), jnp.float32),
        ),
        in_specs=[SMEM] * 4 + [VMEM],
        out_specs=(VMEM, VMEM, VMEM),
        scratch_shapes=[
            pltpu.VMEM((DH, NBLK * BLK), jnp.bfloat16),
            pltpu.VMEM((NBLK, BLK, 256), jnp.float32),
            pltpu.VMEM((DOCS, 8, 256), jnp.float32),
            pltpu.SMEM((NCTX,), jnp.int32),
        ],
        compiler_params=params(),
        cost_estimate=pl.CostEstimate(
            flops=3_000_000_000, bytes_accessed=8_000_000, transcendentals=2_000_000
        ),
        name="attention_backward",
    )(doc_blocks, doc_temp, temp_table, dest, recv)
    dq_recv = lax.all_to_all(
        dq_slots.reshape(NCTX, CAP * BLK, 256), "ctx", split_axis=0, concat_axis=0, tiled=True
    )
    dkv_sum = lax.psum_scatter(
        dkv_part.reshape(GRP * NBLK * QR, 256),
        "ctx",
        scatter_dimension=0,
        axis_index_groups=GROUPS,
        tiled=True,
    ).reshape(NBLK, QR, 256)
    temp_dp = lax.psum(temp_part, "dp")
    dkv_send = pl.pallas_call(
        route_kernel,
        out_shape=jax.ShapeDtypeStruct((NCTX, PAY, 256), jnp.bfloat16),
        in_specs=[SMEM, VMEM, VMEM],
        out_specs=VMEM,
        scratch_shapes=[pltpu.SMEM((NCTX,), jnp.int32)],
        compiler_params=params(),
        name="route_dkv",
    )(dest, dkv_sum, temp_dp)
    dkv_recv = lax.all_to_all(dkv_send, "ctx", split_axis=0, concat_axis=0, tiled=True)
    dq_rows = pl.pallas_call(
        dq_rows_kernel,
        out_shape=jax.ShapeDtypeStruct((1, CAP * BLK, NCTX * 256), jnp.bfloat16),
        in_specs=[VMEM],
        out_specs=VMEM,
        compiler_params=params(),
        cost_estimate=pl.CostEstimate(flops=0, bytes_accessed=6_300_000, transcendentals=0),
        name="dq_rows",
    )(dq_recv)
    dkv_rows, temp_total = pl.pallas_call(
        dkv_rows_kernel,
        out_shape=(
            jax.ShapeDtypeStruct((1, CAP * BLK, 2 * KV * DH), jnp.bfloat16),
            jax.ShapeDtypeStruct((8, 128), jnp.float32),
        ),
        in_specs=[VMEM],
        out_specs=(VMEM, VMEM),
        compiler_params=params(),
        name="dkv_rows",
    )(dkv_recv)
    return dq_rows, dkv_rows, temp_total[0, :TEMPS]


def solution(mesh):
    return jax.shard_map(
        shards,
        mesh=mesh,
        in_specs=(
            P("dp", "ctx", None),
            P("dp", "ctx", None),
            P("dp", "ctx", None),
            P("dp", "ctx", None),
            P("dp", None),
            P("dp", None),
            P(),
            P("dp", None, None),
        ),
        out_specs=(P("dp", "ctx", None), P("dp", "ctx", None), P()),
        check_vma=False,
    )
```

```python
import functools
import math

import jax
import jax.numpy as jnp
from jax import lax
from jax.experimental import pallas as pl
from jax.experimental.pallas import tpu as pltpu
from jax.sharding import PartitionSpec as P

KV = 4
DH = 128
BLK = 128
CAP = 3
NBLK = 16
DOCS = 3
TEMPS = 4
MOSTB = 8
NCTX = 16
GRP = 4
QR = BLK // GRP
HALF = BLK // 2
SEND = CAP * (BLK + QR) + 16
LOG_LEN = [math.log(BLK * n) / math.sqrt(DH) for n in range(1, MOSTB + 1)]
LOG2E = math.log2(math.e)
GROUPS = [[GRP * y + x for x in range(GRP)] for y in range(NCTX // GRP)]
VMEM = pl.BlockSpec(memory_space=pltpu.VMEM)
SMEM = pl.BlockSpec(memory_space=pltpu.SMEM)
HBM = pl.BlockSpec(memory_space=pltpu.HBM)


def pack_kernel(len_ref, temp_ref, dest_ref, table_ref, q_ref, g_ref, k_ref, v_ref, out_ref, meta_ref,
                table_out_ref, k_buf, v_buf, q_buf, g_buf, stage_ref, in_sem, out_sem):
    narrow = [
        pltpu.make_async_copy(src.at[0], buf, in_sem.at[i])
        for i, (src, buf) in enumerate(((k_ref, k_buf), (v_ref, v_buf)))
    ]
    wide = []
    for part in range(GRP):
        cols = pl.ds(part * 1024, 1024)
        for src, buf in ((q_ref, q_buf), (g_ref, g_buf)):
            sem = in_sem.at[2 + len(wide)]
            wide.append(pltpu.make_async_copy(src.at[0, :, cols], buf.at[:, cols], sem))
    for copy in narrow + wide:
        copy.start()
    for d in range(DOCS):
        meta_ref[d] = len_ref[0, d]
        meta_ref[DOCS + d] = temp_ref[0, d]
    for b in range(NBLK):
        meta_ref[2 * DOCS + b] = dest_ref[b]
    for t in range(TEMPS):
        table_out_ref[t] = table_ref[t]
    for copy in narrow:
        copy.wait()
    out = []
    for j in range(NCTX):
        if j % GRP == 0:
            wide[j // GRP * 2].wait()
            wide[j // GRP * 2 + 1].wait()
        head = slice(j // GRP * DH, j // GRP * DH + DH)
        for i, buf in enumerate((k_buf, v_buf)):
            for h in range(2):
                col = (2 * i + h) * DH
                stage_ref[j, BLK : BLK + HALF, col : col + DH] = buf[h * HALF : (h + 1) * HALF, head]
        for i, buf in enumerate((q_buf, g_buf)):
            stage_ref[j, 0:BLK, i * 256 : (i + 1) * 256] = buf[:, j * 256 : (j + 1) * 256]
        out.append(pltpu.make_async_copy(stage_ref.at[j], out_ref.at[j], out_sem.at[j]))
        out[-1].start()
    for copy in out:
        copy.wait()


def pick(index, entries):
    value = entries[0]
    for place in range(1, len(entries)):
        value = jnp.where(index == place, entries[place], value)
    return value


def attention_kernel(meta_ref, table_ref, x_ref, send_ref, part_ref, temp_out_ref, k_ref, v_ref, kt_ref,
                     acc_ref, term_ref, dq_ref, zero_ref, count_ref, rank_ref, sem):
    lens = [meta_ref[d] for d in range(DOCS)]
    ends = [lens[0], lens[0] + lens[1]]
    zero_ref[...] = jnp.zeros_like(zero_ref)
    acc_ref[...] = jnp.zeros_like(acc_ref)
    term_ref[...] = jnp.zeros_like(term_ref)
    for s in range(NCTX):
        count_ref[s] = 0
    for b in range(NBLK):
        shard = meta_ref[2 * DOCS + b]
        rank_ref[b] = jnp.minimum(count_ref[shard], CAP - 1)
        count_ref[shard] += 1
    for s in range(NCTX):
        for r in range(CAP):

            @pl.when(count_ref[s] <= r)
            def _():
                slot = send_ref.at[s, r * BLK : (r + 1) * BLK, :]
                pltpu.make_async_copy(zero_ref, slot, sem.at[0]).start()

    for b in range(NBLK):
        for h in range(2):
            rows = pl.ds(b * BLK + h * HALF, HALF)
            k_ref[rows, :] = x_ref[b, BLK : BLK + HALF, h * 128 : (h + 1) * 128]
            v_ref[rows, :] = x_ref[b, BLK : BLK + HALF, (h + 2) * 128 : (h + 3) * 128]
        kt_ref[:, b * BLK : (b + 1) * BLK] = (
            k_ref[b * BLK : (b + 1) * BLK, :].astype(jnp.float32).T.astype(jnp.bfloat16)
        )

    def block_step(b, carry):
        doc = (b >= ends[0]).astype(jnp.int32) + (b >= ends[1]).astype(jnp.int32)
        start = pick(doc, [0, ends[0], ends[1]])
        width = b - start + 1
        scale = table_ref[meta_ref[DOCS + doc]] * pick(pick(doc, lens) - 1, LOG_LEN)
        shard = meta_ref[2 * DOCS + b]
        own = x_ref[b]
        q_two = jnp.concatenate([own[0:BLK, 0:128], own[0:BLK, 128:256]], axis=0)
        g_two = jnp.concatenate([own[0:BLK, 256:384], own[0:BLK, 384:512]], axis=0)

        def run(n):
            first = pl.multiple_of(start * BLK, BLK)
            k_win = k_ref[pl.ds(first, n * BLK), :]
            v_win = v_ref[pl.ds(first, n * BLK), :]
            contract = (((1,), (1,)), ((), ()))
            raw = lax.dot_general(k_win, q_two, contract, preferred_element_type=jnp.float32)
            dprob = lax.dot_general(v_win, g_two, contract, preferred_element_type=jnp.float32)
            logit = raw * (scale * LOG2E)
            row = lax.broadcasted_iota(jnp.int32, (BLK, 2 * BLK), 0)
            col = lax.broadcasted_iota(jnp.int32, (BLK, 2 * BLK), 1) % BLK
            last = jnp.where(row <= col, logit[(n - 1) * BLK :], -jnp.inf)
            logit = last if n == 1 else jnp.concatenate([logit[: (n - 1) * BLK], last], axis=0)
            top = jnp.max(logit, axis=0, keepdims=True)
            expon = jnp.exp2(logit - top)
            inverse = 1.0 / jnp.sum(expon, axis=0, keepdims=True)
            probs = expon * inverse
            mean = jnp.sum(probs * dprob, axis=0, keepdims=True)
            dlogit = probs * (dprob - mean)
            term_ref[doc] += jnp.sum((dlogit * raw).reshape(-1, 8, 2 * BLK), axis=0)
            scaled = (dlogit * scale).astype(jnp.bfloat16)
            probs_bf = probs.astype(jnp.bfloat16)
            dk = jnp.dot(scaled, q_two, preferred_element_type=jnp.float32)
            dv = jnp.dot(probs_bf, g_two, preferred_element_type=jnp.float32)
            acc_ref[pl.ds(start, n), :, 0:128] += dk.reshape(n, BLK, DH)
            acc_ref[pl.ds(start, n), :, 128:256] += dv.reshape(n, BLK, DH)
            kt_win = kt_ref[:, pl.ds(first, n * BLK)]
            dq_t = jnp.dot(kt_win, scaled, preferred_element_type=jnp.float32)
            dq_ref[b, :, 0:128] = dq_t[:, 0:128].T.astype(jnp.bfloat16)
            dq_ref[b, :, 128:256] = dq_t[:, 128:256].T.astype(jnp.bfloat16)

        for n in range(1, MOSTB + 1):
            pl.when(width == n)(functools.partial(run, n))
        rows = pl.ds(pl.multiple_of(rank_ref[b] * BLK, BLK), BLK)
        pltpu.make_async_copy(dq_ref.at[b], send_ref.at[shard, rows, :], sem.at[0]).start()
        return carry

    lax.fori_loop(0, NBLK, block_step, 0)
    for part in range(GRP):
        for b in range(NBLK):
            part_ref[part, b * QR : (b + 1) * QR, :] = (
                acc_ref[b, part * QR : (part + 1) * QR, :].astype(jnp.bfloat16)
            )
    lane = lax.broadcasted_iota(jnp.int32, (8, 128), 1)
    row = lax.broadcasted_iota(jnp.int32, (8, 128), 0)
    total = jnp.zeros((8, 128), jnp.float32)
    for d in range(DOCS):
        amount = jnp.sum(term_ref[d]) * pick(lens[d] - 1, LOG_LEN)
        total += jnp.where((lane == meta_ref[DOCS + d]) & (row == 0), amount, 0.0)
    temp_out_ref[...] = total
    slots = send_ref.at[:, 0 : CAP * BLK, :]
    pltpu.make_async_copy(slots, slots, sem.at[0]).wait()


def add_kernel(a_ref, b_ref, out_ref):
    out_ref[...] = a_ref[...] + b_ref[...]


def route_kernel(meta_ref, part_ref, temp_ref, held_ref, send_ref, stage_ref, count_ref, sem):
    stage_ref[...] = jnp.zeros_like(stage_ref)
    for s in range(NCTX):
        count_ref[s] = 0
    high = temp_ref[...].astype(jnp.bfloat16).astype(jnp.float32)
    rest = temp_ref[...] - high
    middle = rest.astype(jnp.bfloat16).astype(jnp.float32)
    low = rest - middle
    left = jnp.concatenate([high, middle], axis=0).astype(jnp.bfloat16)
    right = jnp.concatenate([low, jnp.zeros_like(low)], axis=0).astype(jnp.bfloat16)
    for s in range(NCTX):
        stage_ref[s, CAP * QR : CAP * QR + 16, 0:128] = left
        stage_ref[s, CAP * QR : CAP * QR + 16, 128:256] = right
    for b in range(NBLK):
        shard = meta_ref[2 * DOCS + b]
        rank = jnp.minimum(count_ref[shard], CAP - 1)
        count_ref[shard] = rank + 1
        rows = [part_ref[g, b * QR : (b + 1) * QR, :].astype(jnp.float32) for g in range(GRP)]
        total = (rows[0] + rows[1]) + (rows[2] + rows[3])
        stage_ref[shard, pl.ds(pl.multiple_of(rank * QR, QR), QR), :] = total.astype(jnp.bfloat16)
    copy = pltpu.make_async_copy(stage_ref, send_ref.at[:, CAP * BLK : SEND, :], sem.at[0])
    copy.start()
    copy.wait()


def rows_kernel(in_ref, dq_ref, dkv_ref, temp_ref, sem):
    copies = []
    for j in range(NCTX):
        src, dst = in_ref.at[j, 0 : CAP * BLK, :], dq_ref.at[0, :, j * 256 : (j + 1) * 256]
        copies.append(pltpu.make_async_copy(src, dst, sem.at[j]))
        copies[-1].start()
    total = jnp.zeros((8, 128), jnp.float32)
    for j in range(NCTX):
        kv, part = j // GRP, j % GRP
        for r in range(CAP):
            src = pl.ds(CAP * BLK + r * QR, QR)
            dst = pl.ds(r * BLK + part * QR, QR)
            dkv_ref[0, dst, kv * DH : (kv + 1) * DH] = in_ref[j, src, 0:128]
            dkv_ref[0, dst, (KV + kv) * DH : (KV + kv + 1) * DH] = in_ref[j, src, 128:256]
        left = in_ref[j, SEND - 16 : SEND, 0:128].astype(jnp.float32)
        right = in_ref[j, SEND - 16 : SEND, 128:256].astype(jnp.float32)
        total += (left[0:8] + left[8:16]) + right[0:8]
    for t in range(TEMPS):
        temp_ref[t] = total[0, t]
    for copy in copies:
        copy.wait()


def params(mib):
    return pltpu.CompilerParams(vmem_limit_bytes=mib * 1024 * 1024)


def shards(queries, keys, values, out_grad, doc_blocks, doc_temp, temp_table, dest):
    send, meta, table = pl.pallas_call(
        pack_kernel,
        out_shape=(
            jax.ShapeDtypeStruct((NCTX, BLK + HALF, 512), jnp.bfloat16),
            jax.ShapeDtypeStruct((2 * DOCS + NBLK,), jnp.int32),
            jax.ShapeDtypeStruct((TEMPS,), jnp.float32),
        ),
        in_specs=[SMEM] * 4 + [HBM] * 4,
        out_specs=(HBM, SMEM, SMEM),
        scratch_shapes=[
            pltpu.VMEM((BLK, KV * DH), jnp.bfloat16),
            pltpu.VMEM((BLK, KV * DH), jnp.bfloat16),
            pltpu.VMEM((BLK, NCTX * 256), jnp.bfloat16),
            pltpu.VMEM((BLK, NCTX * 256), jnp.bfloat16),
            pltpu.VMEM((NCTX, BLK + HALF, 512), jnp.bfloat16),
            pltpu.SemaphoreType.DMA((2 + 2 * GRP,)),
            pltpu.SemaphoreType.DMA((NCTX,)),
        ],
        compiler_params=params(60),
        name="pack",
    )(doc_blocks, doc_temp, dest.reshape(NBLK), temp_table, queries, out_grad, keys, values)
    recv = lax.all_to_all(send, "ctx", split_axis=0, concat_axis=0, tiled=True)
    dq_send, dkv_part, temp_part = pl.pallas_call(
        attention_kernel,
        out_shape=(
            jax.ShapeDtypeStruct((NCTX, SEND, 256), jnp.bfloat16),
            jax.ShapeDtypeStruct((GRP, NBLK * QR, 256), jnp.bfloat16),
            jax.ShapeDtypeStruct((8, 128), jnp.float32),
        ),
        in_specs=[SMEM] * 2 + [VMEM],
        out_specs=(HBM, VMEM, VMEM),
        scratch_shapes=[
            pltpu.VMEM((NBLK * BLK, DH), jnp.bfloat16),
            pltpu.VMEM((NBLK * BLK, DH), jnp.bfloat16),
            pltpu.VMEM((DH, NBLK * BLK), jnp.bfloat16),
            pltpu.VMEM((NBLK, BLK, 256), jnp.float32),
            pltpu.VMEM((DOCS, 8, 256), jnp.float32),
            pltpu.VMEM((NBLK, BLK, 256), jnp.bfloat16),
            pltpu.VMEM((BLK, 256), jnp.bfloat16),
            pltpu.SMEM((NCTX,), jnp.int32),
            pltpu.SMEM((NBLK,), jnp.int32),
            pltpu.SemaphoreType.DMA((1,)),
        ],
        compiler_params=params(48),
        name="attention_backward",
    )(meta, table, recv)
    dkv_recv = lax.all_to_all(
        dkv_part, "ctx", split_axis=0, concat_axis=0, axis_index_groups=GROUPS, tiled=True
    )
    ndp = lax.axis_size("dp")
    step = 1
    while step < ndp:
        pairs = [(i, i ^ step) for i in range(ndp)]
        temp_part = pl.pallas_call(
            add_kernel,
            out_shape=jax.ShapeDtypeStruct((8, 128), jnp.float32),
            in_specs=[VMEM] * 2,
            out_specs=VMEM,
            compiler_params=params(1),
            name="temp_add",
        )(temp_part, lax.ppermute(temp_part, "dp", pairs))
        step *= 2
    out_send = pl.pallas_call(
        route_kernel,
        out_shape=jax.ShapeDtypeStruct((NCTX, SEND, 256), jnp.bfloat16),
        in_specs=[SMEM, VMEM, VMEM, HBM],
        out_specs=HBM,
        scratch_shapes=[
            pltpu.VMEM((NCTX, CAP * QR + 16, 256), jnp.bfloat16),
            pltpu.SMEM((NCTX,), jnp.int32),
            pltpu.SemaphoreType.DMA((1,)),
        ],
        input_output_aliases={3: 0},
        compiler_params=params(50),
        name="route_dkv",
    )(meta, dkv_recv, temp_part, dq_send)
    out_recv = lax.all_to_all(out_send, "ctx", split_axis=0, concat_axis=0, tiled=True)
    return pl.pallas_call(
        rows_kernel,
        out_shape=(
            jax.ShapeDtypeStruct((1, CAP * BLK, NCTX * 256), jnp.bfloat16),
            jax.ShapeDtypeStruct((1, CAP * BLK, 2 * KV * DH), jnp.bfloat16),
            jax.ShapeDtypeStruct((TEMPS,), jnp.float32),
        ),
        in_specs=[VMEM],
        out_specs=(HBM, VMEM, SMEM),
        scratch_shapes=[pltpu.SemaphoreType.DMA((NCTX,))],
        compiler_params=params(24),
        name="rows",
    )(out_recv)


def solution(mesh):
    return jax.shard_map(
        shards,
        mesh=mesh,
        in_specs=(
            P("dp", "ctx", None),
            P("dp", "ctx", None),
            P("dp", "ctx", None),
            P("dp", "ctx", None),
            P("dp", None),
            P("dp", None),
            P(),
            P("dp", None, None),
        ),
        out_specs=(P("dp", "ctx", None), P("dp", "ctx", None), P()),
        check_vma=False,
    )
```

```python
import functools
import math

import jax
import jax.numpy as jnp
from jax import lax
from jax.experimental import pallas as pl
from jax.experimental.pallas import tpu as pltpu
from jax.sharding import PartitionSpec as P

KV = 4
DH = 128
BLK = 128
CAP = 3
NBLK = 16
DOCS = 3
TEMPS = 4
MOSTB = 8
NCTX = 16
GRP = 4
QR = BLK // GRP
HALF = BLK // 2
SEND = CAP * (BLK + QR) + 16
LOG_LEN = [math.log(BLK * n) / math.sqrt(DH) for n in range(1, MOSTB + 1)]
LOG2E = math.log2(math.e)
MASKED = -1e30
GROUPS = [[GRP * y + x for x in range(GRP)] for y in range(NCTX // GRP)]
VMEM = pl.BlockSpec(memory_space=pltpu.VMEM)
SMEM = pl.BlockSpec(memory_space=pltpu.SMEM)
HBM = pl.BlockSpec(memory_space=pltpu.HBM)


def pack_kernel(len_ref, temp_ref, dest_ref, table_ref, q_ref, g_ref, k_ref, v_ref, out_ref, meta_ref,
                table_out_ref, k_buf, v_buf, q_buf, g_buf, stage_ref, in_sem, out_sem):
    narrow = [
        pltpu.make_async_copy(src.at[0], buf, in_sem.at[i])
        for i, (src, buf) in enumerate(((k_ref, k_buf), (v_ref, v_buf)))
    ]
    wide = []
    for part in range(GRP):
        cols = pl.ds(part * 1024, 1024)
        for src, buf in ((q_ref, q_buf), (g_ref, g_buf)):
            sem = in_sem.at[2 + len(wide)]
            wide.append(pltpu.make_async_copy(src.at[0, :, cols], buf.at[:, cols], sem))
    for copy in narrow + wide:
        copy.start()
    for d in range(DOCS):
        meta_ref[d] = len_ref[0, d]
        meta_ref[DOCS + d] = temp_ref[0, d]
    for b in range(NBLK):
        meta_ref[2 * DOCS + b] = dest_ref[b]
    for t in range(TEMPS):
        table_out_ref[t] = table_ref[t]
    for copy in narrow:
        copy.wait()
    out = []
    for j in range(NCTX):
        if j % GRP == 0:
            wide[j // GRP * 2].wait()
            wide[j // GRP * 2 + 1].wait()
        head = slice(j // GRP * DH, j // GRP * DH + DH)
        for i, buf in enumerate((k_buf, v_buf)):
            for h in range(2):
                col = (2 * i + h) * DH
                stage_ref[j, BLK : BLK + HALF, col : col + DH] = buf[h * HALF : (h + 1) * HALF, head]
        for i, buf in enumerate((q_buf, g_buf)):
            stage_ref[j, 0:BLK, i * 256 : (i + 1) * 256] = buf[:, j * 256 : (j + 1) * 256]
        out.append(pltpu.make_async_copy(stage_ref.at[j], out_ref.at[j], out_sem.at[j]))
        out[-1].start()
    for copy in out:
        copy.wait()


def pick(index, entries):
    value = entries[0]
    for place in range(1, len(entries)):
        value = jnp.where(index == place, entries[place], value)
    return value


def attention_kernel(meta_ref, table_ref, x_ref, send_ref, part_ref, temp_out_ref, k_ref, v_ref, acc_ref,
                     term_ref, dq_ref, zero_ref, count_ref, rank_ref, sem):
    lens = [meta_ref[d] for d in range(DOCS)]
    ends = [lens[0], lens[0] + lens[1]]
    zero_ref[...] = jnp.zeros_like(zero_ref)
    term_ref[...] = jnp.zeros_like(term_ref)
    for s in range(NCTX):
        count_ref[s] = 0
    for b in range(NBLK):
        shard = meta_ref[2 * DOCS + b]
        rank_ref[b] = jnp.minimum(count_ref[shard], CAP - 1)
        count_ref[shard] += 1
    for s in range(NCTX):
        for r in range(CAP):

            @pl.when(count_ref[s] <= r)
            def _():
                slot = send_ref.at[s, r * BLK : (r + 1) * BLK, :]
                pltpu.make_async_copy(zero_ref, slot, sem.at[0]).start()

    for b in range(NBLK):
        for h in range(2):
            rows = pl.ds(b * BLK + h * HALF, HALF)
            k_ref[rows, :] = x_ref[b, BLK : BLK + HALF, h * 128 : (h + 1) * 128]
            v_ref[rows, :] = x_ref[b, BLK : BLK + HALF, (h + 2) * 128 : (h + 3) * 128]

    def block_step(b, carry):
        doc = (b >= ends[0]).astype(jnp.int32) + (b >= ends[1]).astype(jnp.int32)
        start = pick(doc, [0, ends[0], ends[1]])
        width = b - start + 1
        scale = table_ref[meta_ref[DOCS + doc]] * pick(pick(doc, lens) - 1, LOG_LEN)
        end = pick(doc, [ends[0], ends[1], NBLK])

        def rows_of(first, tile):
            parts = []
            for i in range(tile):
                own = x_ref[b + i]
                parts += [own[0:BLK, first : first + 128], own[0:BLK, first + 128 : first + 256]]
            return jnp.concatenate(parts, axis=0)

        def run(n, tile):
            lanes = 2 * BLK * tile
            queries, grads = rows_of(0, tile), rows_of(256, tile)
            first = pl.multiple_of(start * BLK, BLK)
            k_win = k_ref[pl.ds(first, n * BLK), :]
            v_win = v_ref[pl.ds(first, n * BLK), :]
            contract = (((1,), (1,)), ((), ()))
            raw = lax.dot_general(k_win, queries, contract, preferred_element_type=jnp.float32)
            dprob = lax.dot_general(v_win, grads, contract, preferred_element_type=jnp.float32)
            logit = raw * (scale * LOG2E)
            row = lax.broadcasted_iota(jnp.int32, (tile * BLK, lanes), 0)
            col = lax.broadcasted_iota(jnp.int32, (tile * BLK, lanes), 1)
            col = col // (2 * BLK) * BLK + col % BLK
            edge = (n - tile) * BLK
            last = jnp.where(row <= col, logit[edge:], MASKED)
            logit = last if edge == 0 else jnp.concatenate([logit[:edge], last], axis=0)
            top = jnp.max(logit, axis=0, keepdims=True)
            expon = jnp.exp2(logit - top)
            inverse = 1.0 / jnp.sum(expon, axis=0, keepdims=True)
            mean = jnp.sum(expon * dprob, axis=0, keepdims=True) * inverse
            probs = expon * inverse
            dlogit = probs * (dprob - mean)
            term_ref[doc, :, 0:lanes] += jnp.sum((dlogit * logit).reshape(-1, 8, lanes), axis=0)
            scaled = (dlogit * scale).astype(jnp.bfloat16)
            dk = jnp.dot(scaled, queries, preferred_element_type=jnp.float32).reshape(n, BLK, DH)
            dv = jnp.dot(probs.astype(jnp.bfloat16), grads, preferred_element_type=jnp.float32)
            dv = dv.reshape(n, BLK, DH)
            if n > tile:
                acc_ref[pl.ds(start, n - tile), :, 0:128] += dk[: n - tile]
                acc_ref[pl.ds(start, n - tile), :, 128:256] += dv[: n - tile]
            acc_ref[pl.ds(b, tile), :, 0:128] = dk[n - tile :]
            acc_ref[pl.ds(b, tile), :, 128:256] = dv[n - tile :]
            dq = lax.dot_general(
                scaled, k_win, (((0,), (0,)), ((), ())), preferred_element_type=jnp.float32
            ).astype(jnp.bfloat16)
            for i in range(tile):
                dq_ref[b + i, :, 0:128] = dq[2 * i * BLK : (2 * i + 1) * BLK]
                dq_ref[b + i, :, 128:256] = dq[(2 * i + 1) * BLK : (2 * i + 2) * BLK]
                at = pl.ds(pl.multiple_of(rank_ref[b + i] * BLK, BLK), BLK)
                target = send_ref.at[meta_ref[2 * DOCS + b + i], at, :]
                pltpu.make_async_copy(dq_ref.at[b + i], target, sem.at[0]).start()

        for n in range(1, MOSTB + 1, 2):
            pl.when((width == n) & (b + 1 == end))(functools.partial(run, n, 1))
            pl.when((width == n) & (b + 1 < end))(functools.partial(run, n + 1, 2))
        return carry

    lax.fori_loop(0, NBLK, block_step, 0)
    for part in range(GRP):
        for b in range(NBLK):
            part_ref[part, b * QR : (b + 1) * QR, :] = (
                acc_ref[b, part * QR : (part + 1) * QR, :].astype(jnp.bfloat16)
            )
    lane = lax.broadcasted_iota(jnp.int32, (8, 128), 1)
    row = lax.broadcasted_iota(jnp.int32, (8, 128), 0)
    total = jnp.zeros((8, 128), jnp.float32)
    for d in range(DOCS):
        amount = jnp.sum(term_ref[d]) / (table_ref[meta_ref[DOCS + d]] * LOG2E)
        total += jnp.where((lane == meta_ref[DOCS + d]) & (row == 0), amount, 0.0)
    temp_out_ref[...] = total
    slots = send_ref.at[:, 0 : CAP * BLK, :]
    pltpu.make_async_copy(slots, slots, sem.at[0]).wait()


def add_kernel(a_ref, b_ref, out_ref):
    out_ref[...] = a_ref[...] + b_ref[...]


def route_kernel(meta_ref, part_ref, temp_ref, held_ref, send_ref, stage_ref, count_ref, sem):
    stage_ref[...] = jnp.zeros_like(stage_ref)
    for s in range(NCTX):
        count_ref[s] = 0
    high = temp_ref[...].astype(jnp.bfloat16).astype(jnp.float32)
    rest = temp_ref[...] - high
    middle = rest.astype(jnp.bfloat16).astype(jnp.float32)
    low = rest - middle
    left = jnp.concatenate([high, middle], axis=0).astype(jnp.bfloat16)
    right = jnp.concatenate([low, jnp.zeros_like(low)], axis=0).astype(jnp.bfloat16)
    for s in range(NCTX):
        stage_ref[s, CAP * QR : CAP * QR + 16, 0:128] = left
        stage_ref[s, CAP * QR : CAP * QR + 16, 128:256] = right
    for b in range(NBLK):
        shard = meta_ref[2 * DOCS + b]
        rank = jnp.minimum(count_ref[shard], CAP - 1)
        count_ref[shard] = rank + 1
        rows = [part_ref[g, b * QR : (b + 1) * QR, :].astype(jnp.float32) for g in range(GRP)]
        total = (rows[0] + rows[1]) + (rows[2] + rows[3])
        stage_ref[shard, pl.ds(pl.multiple_of(rank * QR, QR), QR), :] = total.astype(jnp.bfloat16)
    copy = pltpu.make_async_copy(stage_ref, send_ref.at[:, CAP * BLK : SEND, :], sem.at[0])
    copy.start()
    copy.wait()


def rows_kernel(in_ref, dq_ref, dkv_ref, temp_ref, sem):
    copies = []
    for j in range(NCTX):
        src, dst = in_ref.at[j, 0 : CAP * BLK, :], dq_ref.at[0, :, j * 256 : (j + 1) * 256]
        copies.append(pltpu.make_async_copy(src, dst, sem.at[j]))
        copies[-1].start()
    total = jnp.zeros((8, 128), jnp.float32)
    for j in range(NCTX):
        kv, part = j // GRP, j % GRP
        for r in range(CAP):
            src = pl.ds(CAP * BLK + r * QR, QR)
            dst = pl.ds(r * BLK + part * QR, QR)
            dkv_ref[0, dst, kv * DH : (kv + 1) * DH] = in_ref[j, src, 0:128]
            dkv_ref[0, dst, (KV + kv) * DH : (KV + kv + 1) * DH] = in_ref[j, src, 128:256]
        left = in_ref[j, SEND - 16 : SEND, 0:128].astype(jnp.float32)
        right = in_ref[j, SEND - 16 : SEND, 128:256].astype(jnp.float32)
        total += (left[0:8] + left[8:16]) + right[0:8]
    for t in range(TEMPS):
        temp_ref[t] = total[0, t]
    for copy in copies:
        copy.wait()


def params(mib):
    return pltpu.CompilerParams(vmem_limit_bytes=mib * 1024 * 1024)


def attention(meta, table, recv):
    return pl.pallas_call(
        attention_kernel,
        out_shape=(
            jax.ShapeDtypeStruct((NCTX, SEND, 256), jnp.bfloat16),
            jax.ShapeDtypeStruct((GRP, NBLK * QR, 256), jnp.bfloat16),
            jax.ShapeDtypeStruct((8, 128), jnp.float32),
        ),
        in_specs=[SMEM] * 2 + [VMEM],
        out_specs=(HBM, VMEM, VMEM),
        scratch_shapes=[
            pltpu.VMEM((NBLK * BLK, DH), jnp.bfloat16),
            pltpu.VMEM((NBLK * BLK, DH), jnp.bfloat16),
            pltpu.VMEM((NBLK, BLK, 256), jnp.float32),
            pltpu.VMEM((DOCS, 8, 512), jnp.float32),
            pltpu.VMEM((NBLK, BLK, 256), jnp.bfloat16),
            pltpu.VMEM((BLK, 256), jnp.bfloat16),
            pltpu.SMEM((NCTX,), jnp.int32),
            pltpu.SMEM((NBLK,), jnp.int32),
            pltpu.SemaphoreType.DMA((1,)),
        ],
        compiler_params=params(48),
        name="attention_backward",
    )(meta, table, recv)


def shards(queries, keys, values, out_grad, doc_blocks, doc_temp, temp_table, dest):
    send, meta, table = pl.pallas_call(
        pack_kernel,
        out_shape=(
            jax.ShapeDtypeStruct((NCTX, BLK + HALF, 512), jnp.bfloat16),
            jax.ShapeDtypeStruct((2 * DOCS + NBLK,), jnp.int32),
            jax.ShapeDtypeStruct((TEMPS,), jnp.float32),
        ),
        in_specs=[SMEM] * 4 + [HBM] * 4,
        out_specs=(HBM, SMEM, SMEM),
        scratch_shapes=[
            pltpu.VMEM((BLK, KV * DH), jnp.bfloat16),
            pltpu.VMEM((BLK, KV * DH), jnp.bfloat16),
            pltpu.VMEM((BLK, NCTX * 256), jnp.bfloat16),
            pltpu.VMEM((BLK, NCTX * 256), jnp.bfloat16),
            pltpu.VMEM((NCTX, BLK + HALF, 512), jnp.bfloat16),
            pltpu.SemaphoreType.DMA((2 + 2 * GRP,)),
            pltpu.SemaphoreType.DMA((NCTX,)),
        ],
        compiler_params=params(60),
        name="pack",
    )(doc_blocks, doc_temp, dest.reshape(NBLK), temp_table, queries, out_grad, keys, values)
    recv = lax.all_to_all(send, "ctx", split_axis=0, concat_axis=0, tiled=True)
    dq_send, dkv_part, temp_part = attention(meta, table, recv)
    dkv_recv = lax.all_to_all(
        dkv_part, "ctx", split_axis=0, concat_axis=0, axis_index_groups=GROUPS, tiled=True
    )
    ndp = lax.axis_size("dp")
    step = 1
    while step < ndp:
        pairs = [(i, i ^ step) for i in range(ndp)]
        temp_part = pl.pallas_call(
            add_kernel,
            out_shape=jax.ShapeDtypeStruct((8, 128), jnp.float32),
            in_specs=[VMEM] * 2,
            out_specs=VMEM,
            compiler_params=params(1),
            name="temp_add",
        )(temp_part, lax.ppermute(temp_part, "dp", pairs))
        step *= 2
    out_send = pl.pallas_call(
        route_kernel,
        out_shape=jax.ShapeDtypeStruct((NCTX, SEND, 256), jnp.bfloat16),
        in_specs=[SMEM, VMEM, VMEM, HBM],
        out_specs=HBM,
        scratch_shapes=[
            pltpu.VMEM((NCTX, CAP * QR + 16, 256), jnp.bfloat16),
            pltpu.SMEM((NCTX,), jnp.int32),
            pltpu.SemaphoreType.DMA((1,)),
        ],
        input_output_aliases={3: 0},
        compiler_params=params(50),
        name="route_dkv",
    )(meta, dkv_recv, temp_part, dq_send)
    out_recv = lax.all_to_all(out_send, "ctx", split_axis=0, concat_axis=0, tiled=True)
    return pl.pallas_call(
        rows_kernel,
        out_shape=(
            jax.ShapeDtypeStruct((1, CAP * BLK, NCTX * 256), jnp.bfloat16),
            jax.ShapeDtypeStruct((1, CAP * BLK, 2 * KV * DH), jnp.bfloat16),
            jax.ShapeDtypeStruct((TEMPS,), jnp.float32),
        ),
        in_specs=[VMEM],
        out_specs=(HBM, VMEM, SMEM),
        scratch_shapes=[pltpu.SemaphoreType.DMA((NCTX,))],
        compiler_params=params(24),
        name="rows",
    )(out_recv)


def solution(mesh):
    return jax.shard_map(
        shards,
        mesh=mesh,
        in_specs=(
            P("dp", "ctx", None),
            P("dp", "ctx", None),
            P("dp", "ctx", None),
            P("dp", "ctx", None),
            P("dp", None),
            P("dp", None),
            P(),
            P("dp", None, None),
        ),
        out_specs=(P("dp", "ctx", None), P("dp", "ctx", None), P()),
        check_vma=False,
    )
```

```python
import functools
import math

import jax
import jax.numpy as jnp
from jax import lax
from jax.experimental import pallas as pl
from jax.experimental.pallas import tpu as pltpu
from jax.sharding import PartitionSpec as P

KV = 4
DH = 128
BLK = 128
CAP = 3
NBLK = 16
DOCS = 3
TEMPS = 4
MOSTB = 8
NCTX = 16
GRP = 4
QR = BLK // GRP
HALF = BLK // 2
SEND = CAP * (BLK + QR) + 16
LOG_LEN = [math.log(BLK * n) / math.sqrt(DH) for n in range(1, MOSTB + 1)]
LOG2E = math.log2(math.e)
MASKED = -1e30
GROUPS = [[GRP * y + x for x in range(GRP)] for y in range(NCTX // GRP)]
VMEM = pl.BlockSpec(memory_space=pltpu.VMEM)
SMEM = pl.BlockSpec(memory_space=pltpu.SMEM)
HBM = pl.BlockSpec(memory_space=pltpu.HBM)


def pack_kernel(len_hbm, temp_hbm, dest_hbm, table_hbm, q_ref, g_ref, k_ref, v_ref, out_ref, meta_ref,
                table_out_ref, k_buf, v_buf, q_buf, g_buf, len_ref, temp_ref, dest_ref, table_ref,
                in_sem):
    narrow = [
        pltpu.make_async_copy(src.at[0], buf, in_sem.at[i])
        for i, (src, buf) in enumerate(((k_ref, k_buf), (v_ref, v_buf)))
    ]
    wide = []
    for part in range(GRP):
        cols = pl.ds(part * 1024, 1024)
        for src, buf in ((q_ref, q_buf), (g_ref, g_buf)):
            sem = in_sem.at[2 + len(wide)]
            wide.append(pltpu.make_async_copy(src.at[0, :, cols], buf.at[:, cols], sem))
    small = [
        pltpu.make_async_copy(src, buf, in_sem.at[2 + len(wide) + i])
        for i, (src, buf) in enumerate(
            ((len_hbm, len_ref), (temp_hbm, temp_ref), (dest_hbm, dest_ref), (table_hbm, table_ref))
        )
    ]
    for copy in narrow + wide + small:
        copy.start()
    for copy in small:
        copy.wait()
    for d in range(DOCS):
        meta_ref[d] = len_ref[0, d]
        meta_ref[DOCS + d] = temp_ref[0, d]
    for b in range(NBLK):
        meta_ref[2 * DOCS + b] = dest_ref[b]
    for t in range(TEMPS):
        table_out_ref[t] = table_ref[t]
    for copy in narrow:
        copy.wait()
    for j in range(NCTX):
        if j % GRP == 0:
            wide[j // GRP * 2].wait()
            wide[j // GRP * 2 + 1].wait()
        head = slice(j // GRP * DH, j // GRP * DH + DH)
        for i, buf in enumerate((k_buf, v_buf)):
            for h in range(2):
                col = (2 * i + h) * DH
                out_ref[j, BLK : BLK + HALF, col : col + DH] = buf[h * HALF : (h + 1) * HALF, head]
        for i, buf in enumerate((q_buf, g_buf)):
            out_ref[j, 0:BLK, i * 256 : (i + 1) * 256] = buf[:, j * 256 : (j + 1) * 256]


def pick(index, entries):
    value = entries[0]
    for place in range(1, len(entries)):
        value = jnp.where(index == place, entries[place], value)
    return value


def attention_kernel(meta_ref, table_ref, x_ref, send_ref, part_ref, temp_out_ref, k_ref, v_ref, acc_ref,
                     term_ref, dq_ref, zero_ref, count_ref, rank_ref, sem):
    lens = [meta_ref[d] for d in range(DOCS)]
    ends = [lens[0], lens[0] + lens[1]]
    zero_ref[...] = jnp.zeros_like(zero_ref)
    term_ref[...] = jnp.zeros_like(term_ref)
    for s in range(NCTX):
        count_ref[s] = 0
    for b in range(NBLK):
        shard = meta_ref[2 * DOCS + b]
        rank_ref[b] = jnp.minimum(count_ref[shard], CAP - 1)
        count_ref[shard] += 1
    for s in range(NCTX):
        for r in range(CAP):

            @pl.when(count_ref[s] <= r)
            def _():
                slot = send_ref.at[s, r * BLK : (r + 1) * BLK, :]
                pltpu.make_async_copy(zero_ref, slot, sem.at[0]).start()

    for b in range(NBLK):
        for h in range(2):
            rows = pl.ds(b * BLK + h * HALF, HALF)
            k_ref[rows, :] = x_ref[b, BLK : BLK + HALF, h * 128 : (h + 1) * 128]
            v_ref[rows, :] = x_ref[b, BLK : BLK + HALF, (h + 2) * 128 : (h + 3) * 128]

    def block_step(b, carry):
        doc = (b >= ends[0]).astype(jnp.int32) + (b >= ends[1]).astype(jnp.int32)
        start = pick(doc, [0, ends[0], ends[1]])
        width = b - start + 1
        scale = table_ref[meta_ref[DOCS + doc]] * pick(pick(doc, lens) - 1, LOG_LEN)
        end = pick(doc, [ends[0], ends[1], NBLK])

        def rows_of(first, tile):
            parts = []
            for i in range(tile):
                own = x_ref[b + i]
                parts += [own[0:BLK, first : first + 128], own[0:BLK, first + 128 : first + 256]]
            return jnp.concatenate(parts, axis=0)

        def run(n, tile):
            lanes = 2 * BLK * tile
            queries, grads = rows_of(0, tile), rows_of(256, tile)
            first = pl.multiple_of(start * BLK, BLK)
            k_win = k_ref[pl.ds(first, n * BLK), :]
            v_win = v_ref[pl.ds(first, n * BLK), :]
            contract = (((1,), (1,)), ((), ()))
            raw = lax.dot_general(k_win, queries, contract, preferred_element_type=jnp.float32)
            dprob = lax.dot_general(v_win, grads, contract, preferred_element_type=jnp.float32)
            logit = raw * (scale * LOG2E)
            row = lax.broadcasted_iota(jnp.int32, (tile * BLK, lanes), 0)
            col = lax.broadcasted_iota(jnp.int32, (tile * BLK, lanes), 1)
            col = col // (2 * BLK) * BLK + col % BLK
            edge = (n - tile) * BLK
            last = jnp.where(row <= col, logit[edge:], MASKED)
            logit = last if edge == 0 else jnp.concatenate([logit[:edge], last], axis=0)
            top = jnp.max(logit, axis=0, keepdims=True)
            expon = jnp.exp2(logit - top)
            inverse = 1.0 / jnp.sum(expon, axis=0, keepdims=True)
            mean = jnp.sum(expon * dprob, axis=0, keepdims=True) * inverse
            probs = expon * inverse
            dlogit = probs * (dprob - mean)
            term_ref[doc, :, 0:lanes] += jnp.sum((dlogit * logit).reshape(-1, 8, lanes), axis=0)
            scaled = (dlogit * scale).astype(jnp.bfloat16)
            dk = jnp.dot(scaled, queries, preferred_element_type=jnp.float32).reshape(n, BLK, DH)
            dv = jnp.dot(probs.astype(jnp.bfloat16), grads, preferred_element_type=jnp.float32)
            dv = dv.reshape(n, BLK, DH)
            if n > tile:
                acc_ref[pl.ds(start, n - tile), :, 0:128] += dk[: n - tile]
                acc_ref[pl.ds(start, n - tile), :, 128:256] += dv[: n - tile]
            acc_ref[pl.ds(b, tile), :, 0:128] = dk[n - tile :]
            acc_ref[pl.ds(b, tile), :, 128:256] = dv[n - tile :]
            dq = lax.dot_general(
                scaled, k_win, (((0,), (0,)), ((), ())), preferred_element_type=jnp.float32
            ).astype(jnp.bfloat16)
            for i in range(tile):
                dq_ref[b + i, :, 0:128] = dq[2 * i * BLK : (2 * i + 1) * BLK]
                dq_ref[b + i, :, 128:256] = dq[(2 * i + 1) * BLK : (2 * i + 2) * BLK]
                at = pl.ds(pl.multiple_of(rank_ref[b + i] * BLK, BLK), BLK)
                target = send_ref.at[meta_ref[2 * DOCS + b + i], at, :]
                pltpu.make_async_copy(dq_ref.at[b + i], target, sem.at[0]).start()

        for n in range(1, MOSTB + 1, 2):
            pl.when((width == n) & (b + 1 == end))(functools.partial(run, n, 1))
            pl.when((width == n) & (b + 1 < end))(functools.partial(run, n + 1, 2))
        return carry

    lax.fori_loop(0, NBLK, block_step, 0)
    for part in range(GRP):
        for b in range(NBLK):
            part_ref[part, b * QR : (b + 1) * QR, :] = (
                acc_ref[b, part * QR : (part + 1) * QR, :].astype(jnp.bfloat16)
            )
    lane = lax.broadcasted_iota(jnp.int32, (8, 128), 1)
    row = lax.broadcasted_iota(jnp.int32, (8, 128), 0)
    total = jnp.zeros((8, 128), jnp.float32)
    for d in range(DOCS):
        amount = jnp.sum(term_ref[d]) / (table_ref[meta_ref[DOCS + d]] * LOG2E)
        total += jnp.where((lane == meta_ref[DOCS + d]) & (row == 0), amount, 0.0)
    temp_out_ref[...] = total
    slots = send_ref.at[:, 0 : CAP * BLK, :]
    pltpu.make_async_copy(slots, slots, sem.at[0]).wait()


def add_kernel(a_ref, b_ref, out_ref):
    out_ref[...] = a_ref[...] + b_ref[...]


def route_kernel(meta_ref, part_ref, temp_ref, held_ref, send_ref, stage_ref, count_ref, sem):
    stage_ref[...] = jnp.zeros_like(stage_ref)
    for s in range(NCTX):
        count_ref[s] = 0
    high = temp_ref[...].astype(jnp.bfloat16).astype(jnp.float32)
    rest = temp_ref[...] - high
    middle = rest.astype(jnp.bfloat16).astype(jnp.float32)
    low = rest - middle
    left = jnp.concatenate([high, middle], axis=0).astype(jnp.bfloat16)
    right = jnp.concatenate([low, jnp.zeros_like(low)], axis=0).astype(jnp.bfloat16)
    for s in range(NCTX):
        stage_ref[s, CAP * QR : CAP * QR + 16, 0:128] = left
        stage_ref[s, CAP * QR : CAP * QR + 16, 128:256] = right
    for b in range(NBLK):
        shard = meta_ref[2 * DOCS + b]
        rank = jnp.minimum(count_ref[shard], CAP - 1)
        count_ref[shard] = rank + 1
        rows = [part_ref[g, b * QR : (b + 1) * QR, :].astype(jnp.float32) for g in range(GRP)]
        total = (rows[0] + rows[1]) + (rows[2] + rows[3])
        stage_ref[shard, pl.ds(pl.multiple_of(rank * QR, QR), QR), :] = total.astype(jnp.bfloat16)
    copy = pltpu.make_async_copy(stage_ref, send_ref.at[:, CAP * BLK : SEND, :], sem.at[0])
    copy.start()
    copy.wait()


def rows_kernel(in_ref, dq_ref, dkv_ref, temp_ref, sem):
    copies = []
    for j in range(NCTX):
        src, dst = in_ref.at[j, 0 : CAP * BLK, :], dq_ref.at[0, :, j * 256 : (j + 1) * 256]
        copies.append(pltpu.make_async_copy(src, dst, sem.at[j]))
        copies[-1].start()
    total = jnp.zeros((8, 128), jnp.float32)
    for j in range(NCTX):
        kv, part = j // GRP, j % GRP
        for r in range(CAP):
            src = pl.ds(CAP * BLK + r * QR, QR)
            dst = pl.ds(r * BLK + part * QR, QR)
            dkv_ref[0, dst, kv * DH : (kv + 1) * DH] = in_ref[j, src, 0:128]
            dkv_ref[0, dst, (KV + kv) * DH : (KV + kv + 1) * DH] = in_ref[j, src, 128:256]
        left = in_ref[j, SEND - 16 : SEND, 0:128].astype(jnp.float32)
        right = in_ref[j, SEND - 16 : SEND, 128:256].astype(jnp.float32)
        total += (left[0:8] + left[8:16]) + right[0:8]
    for t in range(TEMPS):
        temp_ref[t] = total[0, t]
    for copy in copies:
        copy.wait()


def params(mib):
    return pltpu.CompilerParams(vmem_limit_bytes=mib * 1024 * 1024)


def attention(meta, table, recv):
    return pl.pallas_call(
        attention_kernel,
        out_shape=(
            jax.ShapeDtypeStruct((NCTX, SEND, 256), jnp.bfloat16),
            jax.ShapeDtypeStruct((GRP, NBLK * QR, 256), jnp.bfloat16),
            jax.ShapeDtypeStruct((8, 128), jnp.float32),
        ),
        in_specs=[SMEM] * 2 + [VMEM],
        out_specs=(HBM, VMEM, VMEM),
        scratch_shapes=[
            pltpu.VMEM((NBLK * BLK, DH), jnp.bfloat16),
            pltpu.VMEM((NBLK * BLK, DH), jnp.bfloat16),
            pltpu.VMEM((NBLK, BLK, 256), jnp.float32),
            pltpu.VMEM((DOCS, 8, 512), jnp.float32),
            pltpu.VMEM((NBLK, BLK, 256), jnp.bfloat16),
            pltpu.VMEM((BLK, 256), jnp.bfloat16),
            pltpu.SMEM((NCTX,), jnp.int32),
            pltpu.SMEM((NBLK,), jnp.int32),
            pltpu.SemaphoreType.DMA((1,)),
        ],
        compiler_params=params(48),
        name="attention_backward",
    )(meta, table, recv)


def shards(queries, keys, values, out_grad, doc_blocks, doc_temp, temp_table, dest):
    send, meta, table = pl.pallas_call(
        pack_kernel,
        out_shape=(
            jax.ShapeDtypeStruct((NCTX, BLK + HALF, 512), jnp.bfloat16),
            jax.ShapeDtypeStruct((2 * DOCS + NBLK,), jnp.int32),
            jax.ShapeDtypeStruct((TEMPS,), jnp.float32),
        ),
        in_specs=[HBM] * 8,
        out_specs=(VMEM, SMEM, SMEM),
        scratch_shapes=[
            pltpu.VMEM((BLK, KV * DH), jnp.bfloat16),
            pltpu.VMEM((BLK, KV * DH), jnp.bfloat16),
            pltpu.VMEM((BLK, NCTX * 256), jnp.bfloat16),
            pltpu.VMEM((BLK, NCTX * 256), jnp.bfloat16),
            pltpu.SMEM((1, DOCS), jnp.int32),
            pltpu.SMEM((1, DOCS), jnp.int32),
            pltpu.SMEM((NBLK,), jnp.int32),
            pltpu.SMEM((TEMPS,), jnp.float32),
            pltpu.SemaphoreType.DMA((6 + 2 * GRP,)),
        ],
        compiler_params=params(24),
        name="pack",
    )(
        *[
            pltpu.with_memory_space_constraint(a, pltpu.HBM)
            for a in (doc_blocks, doc_temp, dest.reshape(NBLK), temp_table, queries, out_grad, keys, values)
        ]
    )
    recv = lax.all_to_all(send, "ctx", split_axis=0, concat_axis=0, tiled=True)
    dq_send, dkv_part, temp_part = attention(meta, table, recv)
    dkv_recv = lax.all_to_all(
        dkv_part, "ctx", split_axis=0, concat_axis=0, axis_index_groups=GROUPS, tiled=True
    )
    ndp = lax.axis_size("dp")
    step = 1
    while step < ndp:
        pairs = [(i, i ^ step) for i in range(ndp)]
        temp_part = pl.pallas_call(
            add_kernel,
            out_shape=jax.ShapeDtypeStruct((8, 128), jnp.float32),
            in_specs=[VMEM] * 2,
            out_specs=VMEM,
            compiler_params=params(1),
            name="temp_add",
        )(temp_part, lax.ppermute(temp_part, "dp", pairs))
        step *= 2
    out_send = pl.pallas_call(
        route_kernel,
        out_shape=jax.ShapeDtypeStruct((NCTX, SEND, 256), jnp.bfloat16),
        in_specs=[SMEM, VMEM, VMEM, HBM],
        out_specs=HBM,
        scratch_shapes=[
            pltpu.VMEM((NCTX, CAP * QR + 16, 256), jnp.bfloat16),
            pltpu.SMEM((NCTX,), jnp.int32),
            pltpu.SemaphoreType.DMA((1,)),
        ],
        input_output_aliases={3: 0},
        compiler_params=params(50),
        name="route_dkv",
    )(meta, dkv_recv, temp_part, dq_send)
    out_recv = lax.all_to_all(out_send, "ctx", split_axis=0, concat_axis=0, tiled=True)
    return pl.pallas_call(
        rows_kernel,
        out_shape=(
            jax.ShapeDtypeStruct((1, CAP * BLK, NCTX * 256), jnp.bfloat16),
            jax.ShapeDtypeStruct((1, CAP * BLK, 2 * KV * DH), jnp.bfloat16),
            jax.ShapeDtypeStruct((TEMPS,), jnp.float32),
        ),
        in_specs=[VMEM],
        out_specs=(HBM, VMEM, SMEM),
        scratch_shapes=[pltpu.SemaphoreType.DMA((NCTX,))],
        compiler_params=params(24),
        name="rows",
    )(out_recv)


def solution(mesh):
    return jax.shard_map(
        shards,
        mesh=mesh,
        in_specs=(
            P("dp", "ctx", None),
            P("dp", "ctx", None),
            P("dp", "ctx", None),
            P("dp", "ctx", None),
            P("dp", None),
            P("dp", None),
            P(),
            P("dp", None, None),
        ),
        out_specs=(P("dp", "ctx", None), P("dp", "ctx", None), P()),
        check_vma=False,
    )
```

```python
import functools
import math

import jax
import jax.numpy as jnp
from jax import lax
from jax.experimental import pallas as pl
from jax.experimental.pallas import tpu as pltpu
from jax.sharding import PartitionSpec as P

KV = 4
DH = 128
BLK = 128
CAP = 3
NBLK = 16
DOCS = 3
TEMPS = 4
MOSTB = 8
NCTX = 16
GRP = 4
QR = BLK // GRP
HALF = BLK // 2
SEND = CAP * (BLK + QR) + 16
LOG_LEN = [math.log(BLK * n) / math.sqrt(DH) for n in range(1, MOSTB + 1)]
LOG2E = math.log2(math.e)
MASKED = -1e30
GROUPS = [[GRP * y + x for x in range(GRP)] for y in range(NCTX // GRP)]
VMEM = pl.BlockSpec(memory_space=pltpu.VMEM)
SMEM = pl.BlockSpec(memory_space=pltpu.SMEM)
HBM = pl.BlockSpec(memory_space=pltpu.HBM)


def pack_kernel(len_hbm, temp_hbm, dest_hbm, table_hbm, q_ref, g_ref, k_ref, v_ref, out_ref, meta_ref,
                table_out_ref, k_buf, v_buf, q_buf, g_buf, len_ref, temp_ref, dest_ref, table_ref,
                in_sem):
    narrow = [
        pltpu.make_async_copy(src.at[0], buf, in_sem.at[i])
        for i, (src, buf) in enumerate(((k_ref, k_buf), (v_ref, v_buf)))
    ]
    wide = []
    for part in range(GRP):
        cols = pl.ds(part * 1024, 1024)
        for src, buf in ((q_ref, q_buf), (g_ref, g_buf)):
            sem = in_sem.at[2 + len(wide)]
            wide.append(pltpu.make_async_copy(src.at[0, :, cols], buf.at[:, cols], sem))
    small = [
        pltpu.make_async_copy(src, buf, in_sem.at[2 + len(wide) + i])
        for i, (src, buf) in enumerate(
            ((len_hbm, len_ref), (temp_hbm, temp_ref), (dest_hbm, dest_ref), (table_hbm, table_ref))
        )
    ]
    for copy in narrow + wide + small:
        copy.start()
    for copy in small:
        copy.wait()
    for d in range(DOCS):
        meta_ref[d] = len_ref[0, d]
        meta_ref[DOCS + d] = temp_ref[0, d]
    for b in range(NBLK):
        meta_ref[2 * DOCS + b] = dest_ref[b]
    for t in range(TEMPS):
        table_out_ref[t] = table_ref[t]
    for copy in narrow:
        copy.wait()
    for j in range(NCTX):
        if j % GRP == 0:
            wide[j // GRP * 2].wait()
            wide[j // GRP * 2 + 1].wait()
        head = slice(j // GRP * DH, j // GRP * DH + DH)
        for i, buf in enumerate((k_buf, v_buf)):
            for h in range(2):
                col = (2 * i + h) * DH
                out_ref[j, BLK : BLK + HALF, col : col + DH] = buf[h * HALF : (h + 1) * HALF, head]
        for i, buf in enumerate((q_buf, g_buf)):
            out_ref[j, 0:BLK, i * 256 : (i + 1) * 256] = buf[:, j * 256 : (j + 1) * 256]


def pick(index, entries):
    value = entries[0]
    for place in range(1, len(entries)):
        value = jnp.where(index == place, entries[place], value)
    return value


def attention_kernel(meta_ref, table_ref, x_ref, send_ref, part_out, temp_out_ref, k_ref, v_ref, acc_ref,
                     term_ref, dq_ref, zero_ref, part_ref, count_ref, rank_ref, sem):
    lens = [meta_ref[d] for d in range(DOCS)]
    ends = [lens[0], lens[0] + lens[1]]
    zero_ref[...] = jnp.zeros_like(zero_ref)
    term_ref[...] = jnp.zeros_like(term_ref)
    for s in range(NCTX):
        count_ref[s] = 0
    for b in range(NBLK):
        shard = meta_ref[2 * DOCS + b]
        rank_ref[b] = jnp.minimum(count_ref[shard], CAP - 1)
        count_ref[shard] += 1
    for s in range(NCTX):
        for r in range(CAP):

            @pl.when(count_ref[s] <= r)
            def _():
                slot = send_ref.at[s, r * BLK : (r + 1) * BLK, :]
                pltpu.make_async_copy(zero_ref, slot, sem.at[0]).start()

    for b in range(NBLK):
        for h in range(2):
            rows = pl.ds(b * BLK + h * HALF, HALF)
            k_ref[rows, :] = x_ref[b, BLK : BLK + HALF, h * 128 : (h + 1) * 128]
            v_ref[rows, :] = x_ref[b, BLK : BLK + HALF, (h + 2) * 128 : (h + 3) * 128]

    def block_step(b, carry):
        doc = (b >= ends[0]).astype(jnp.int32) + (b >= ends[1]).astype(jnp.int32)
        start = pick(doc, [0, ends[0], ends[1]])
        width = b - start + 1
        scale = table_ref[meta_ref[DOCS + doc]] * pick(pick(doc, lens) - 1, LOG_LEN)
        end = pick(doc, [ends[0], ends[1], NBLK])

        def rows_of(first, tile):
            parts = []
            for i in range(tile):
                own = x_ref[b + i]
                parts += [own[0:BLK, first : first + 128], own[0:BLK, first + 128 : first + 256]]
            return jnp.concatenate(parts, axis=0)

        def run(n, tile):
            lanes = 2 * BLK * tile
            queries, grads = rows_of(0, tile), rows_of(256, tile)
            first = pl.multiple_of(start * BLK, BLK)
            k_win = k_ref[pl.ds(first, n * BLK), :]
            v_win = v_ref[pl.ds(first, n * BLK), :]
            contract = (((1,), (1,)), ((), ()))
            raw = lax.dot_general(k_win, queries, contract, preferred_element_type=jnp.float32)
            dprob = lax.dot_general(v_win, grads, contract, preferred_element_type=jnp.float32)
            logit = raw * (scale * LOG2E)
            row = lax.broadcasted_iota(jnp.int32, (tile * BLK, lanes), 0)
            col = lax.broadcasted_iota(jnp.int32, (tile * BLK, lanes), 1)
            col = col // (2 * BLK) * BLK + col % BLK
            edge = (n - tile) * BLK
            last = jnp.where(row <= col, logit[edge:], MASKED)
            logit = last if edge == 0 else jnp.concatenate([logit[:edge], last], axis=0)
            top = jnp.max(logit, axis=0, keepdims=True)
            expon = jnp.exp2(logit - top)
            inverse = 1.0 / jnp.sum(expon, axis=0, keepdims=True)
            mean = jnp.sum(expon * dprob, axis=0, keepdims=True) * inverse
            probs = expon * inverse
            dv = jnp.dot(probs.astype(jnp.bfloat16), grads, preferred_element_type=jnp.float32)
            dv = dv.reshape(n, BLK, DH)
            dlogit = probs * (dprob - mean)
            term_ref[doc, :, 0:lanes] += jnp.sum((dlogit * logit).reshape(-1, 8, lanes), axis=0)
            scaled = (dlogit * scale).astype(jnp.bfloat16)
            dk = jnp.dot(scaled, queries, preferred_element_type=jnp.float32).reshape(n, BLK, DH)
            if n > tile:
                acc_ref[pl.ds(start, n - tile), :, 0:128] += dk[: n - tile]
                acc_ref[pl.ds(start, n - tile), :, 128:256] += dv[: n - tile]
            acc_ref[pl.ds(b, tile), :, 0:128] = dk[n - tile :]
            acc_ref[pl.ds(b, tile), :, 128:256] = dv[n - tile :]
            dq = lax.dot_general(
                scaled, k_win, (((0,), (0,)), ((), ())), preferred_element_type=jnp.float32
            ).astype(jnp.bfloat16)
            for i in range(tile):
                dq_ref[b + i, :, 0:128] = dq[2 * i * BLK : (2 * i + 1) * BLK]
                dq_ref[b + i, :, 128:256] = dq[(2 * i + 1) * BLK : (2 * i + 2) * BLK]
                at = pl.ds(pl.multiple_of(rank_ref[b + i] * BLK, BLK), BLK)
                target = send_ref.at[meta_ref[2 * DOCS + b + i], at, :]
                pltpu.make_async_copy(dq_ref.at[b + i], target, sem.at[0]).start()

        for n in range(1, MOSTB + 1, 2):
            pl.when((width == n) & (b + 1 == end))(functools.partial(run, n, 1))
            pl.when((width == n) & (b + 1 < end))(functools.partial(run, n + 1, 2))
        return carry

    lax.fori_loop(0, NBLK, block_step, 0)
    parts = []
    for part in range(GRP):
        for b in range(NBLK):
            part_ref[part, b * QR : (b + 1) * QR, :] = (
                acc_ref[b, part * QR : (part + 1) * QR, :].astype(jnp.bfloat16)
            )
        parts.append(pltpu.make_async_copy(part_ref.at[part], part_out.at[part], sem.at[1 + part]))
        parts[-1].start()
    lane = lax.broadcasted_iota(jnp.int32, (8, 128), 1)
    row = lax.broadcasted_iota(jnp.int32, (8, 128), 0)
    total = jnp.zeros((8, 128), jnp.float32)
    for d in range(DOCS):
        amount = jnp.sum(term_ref[d]) / (table_ref[meta_ref[DOCS + d]] * LOG2E)
        total += jnp.where((lane == meta_ref[DOCS + d]) & (row == 0), amount, 0.0)
    temp_out_ref[...] = total
    for copy in parts:
        copy.wait()
    slots = send_ref.at[:, 0 : CAP * BLK, :]
    pltpu.make_async_copy(slots, slots, sem.at[0]).wait()


def add_kernel(a_ref, b_ref, out_ref):
    out_ref[...] = a_ref[...] + b_ref[...]


def route_kernel(meta_ref, part_ref, temp_ref, held_ref, send_ref, stage_ref, count_ref, sem):
    stage_ref[...] = jnp.zeros_like(stage_ref)
    for s in range(NCTX):
        count_ref[s] = 0
    high = temp_ref[...].astype(jnp.bfloat16).astype(jnp.float32)
    rest = temp_ref[...] - high
    middle = rest.astype(jnp.bfloat16).astype(jnp.float32)
    low = rest - middle
    left = jnp.concatenate([high, middle], axis=0).astype(jnp.bfloat16)
    right = jnp.concatenate([low, jnp.zeros_like(low)], axis=0).astype(jnp.bfloat16)
    for s in range(NCTX):
        stage_ref[s, CAP * QR : CAP * QR + 16, 0:128] = left
        stage_ref[s, CAP * QR : CAP * QR + 16, 128:256] = right
    for b in range(NBLK):
        shard = meta_ref[2 * DOCS + b]
        rank = jnp.minimum(count_ref[shard], CAP - 1)
        count_ref[shard] = rank + 1
        rows = [part_ref[g, b * QR : (b + 1) * QR, :].astype(jnp.float32) for g in range(GRP)]
        total = (rows[0] + rows[1]) + (rows[2] + rows[3])
        stage_ref[shard, pl.ds(pl.multiple_of(rank * QR, QR), QR), :] = total.astype(jnp.bfloat16)
    copy = pltpu.make_async_copy(stage_ref, send_ref.at[:, CAP * BLK : SEND, :], sem.at[0])
    copy.start()
    copy.wait()


def rows_kernel(in_ref, dq_ref, dkv_ref, temp_ref, stage_ref, sem):
    copies = []
    for r in range(2 * CAP):
        rows = slice(r * BLK // 2, (r + 1) * BLK // 2)
        for j in range(NCTX):
            stage_ref[rows, j * 256 : (j + 1) * 256] = in_ref[j, rows, :]
        copies.append(pltpu.make_async_copy(stage_ref.at[rows], dq_ref.at[0, rows], sem.at[r]))
        copies[-1].start()
    total = jnp.zeros((8, 128), jnp.float32)
    for j in range(NCTX):
        kv, part = j // GRP, j % GRP
        for r in range(CAP):
            src = pl.ds(CAP * BLK + r * QR, QR)
            dst = pl.ds(r * BLK + part * QR, QR)
            dkv_ref[0, dst, kv * DH : (kv + 1) * DH] = in_ref[j, src, 0:128]
            dkv_ref[0, dst, (KV + kv) * DH : (KV + kv + 1) * DH] = in_ref[j, src, 128:256]
        left = in_ref[j, SEND - 16 : SEND, 0:128].astype(jnp.float32)
        right = in_ref[j, SEND - 16 : SEND, 128:256].astype(jnp.float32)
        total += (left[0:8] + left[8:16]) + right[0:8]
    for t in range(TEMPS):
        temp_ref[t] = total[0, t]
    for copy in copies:
        copy.wait()


def params(mib):
    return pltpu.CompilerParams(vmem_limit_bytes=mib * 1024 * 1024)


def attention(meta, table, recv):
    return pl.pallas_call(
        attention_kernel,
        out_shape=(
            jax.ShapeDtypeStruct((NCTX, SEND, 256), jnp.bfloat16),
            jax.ShapeDtypeStruct((GRP, NBLK * QR, 256), jnp.bfloat16),
            jax.ShapeDtypeStruct((8, 128), jnp.float32),
        ),
        in_specs=[SMEM] * 2 + [VMEM],
        out_specs=(HBM, HBM, VMEM),
        scratch_shapes=[
            pltpu.VMEM((NBLK * BLK, DH), jnp.bfloat16),
            pltpu.VMEM((NBLK * BLK, DH), jnp.bfloat16),
            pltpu.VMEM((NBLK, BLK, 256), jnp.float32),
            pltpu.VMEM((DOCS, 8, 512), jnp.float32),
            pltpu.VMEM((NBLK, BLK, 256), jnp.bfloat16),
            pltpu.VMEM((BLK, 256), jnp.bfloat16),
            pltpu.VMEM((GRP, NBLK * QR, 256), jnp.bfloat16),
            pltpu.SMEM((NCTX,), jnp.int32),
            pltpu.SMEM((NBLK,), jnp.int32),
            pltpu.SemaphoreType.DMA((1 + GRP,)),
        ],
        compiler_params=params(48),
        name="attention_backward",
    )(meta, table, recv)


def shards(queries, keys, values, out_grad, doc_blocks, doc_temp, temp_table, dest):
    send, meta, table = pl.pallas_call(
        pack_kernel,
        out_shape=(
            jax.ShapeDtypeStruct((NCTX, BLK + HALF, 512), jnp.bfloat16),
            jax.ShapeDtypeStruct((2 * DOCS + NBLK,), jnp.int32),
            jax.ShapeDtypeStruct((TEMPS,), jnp.float32),
        ),
        in_specs=[HBM] * 8,
        out_specs=(VMEM, SMEM, SMEM),
        scratch_shapes=[
            pltpu.VMEM((BLK, KV * DH), jnp.bfloat16),
            pltpu.VMEM((BLK, KV * DH), jnp.bfloat16),
            pltpu.VMEM((BLK, NCTX * 256), jnp.bfloat16),
            pltpu.VMEM((BLK, NCTX * 256), jnp.bfloat16),
            pltpu.SMEM((1, DOCS), jnp.int32),
            pltpu.SMEM((1, DOCS), jnp.int32),
            pltpu.SMEM((NBLK,), jnp.int32),
            pltpu.SMEM((TEMPS,), jnp.float32),
            pltpu.SemaphoreType.DMA((6 + 2 * GRP,)),
        ],
        compiler_params=params(24),
        name="pack",
    )(
        *[
            pltpu.with_memory_space_constraint(a, pltpu.HBM)
            for a in (doc_blocks, doc_temp, dest.reshape(NBLK), temp_table, queries, out_grad, keys, values)
        ]
    )
    recv = lax.all_to_all(send, "ctx", split_axis=0, concat_axis=0, tiled=True)
    dq_send, dkv_part, temp_part = attention(meta, table, recv)
    dkv_recv = lax.all_to_all(
        dkv_part, "ctx", split_axis=0, concat_axis=0, axis_index_groups=GROUPS, tiled=True
    )
    ndp = lax.axis_size("dp")
    step = 1
    while step < ndp:
        pairs = [(i, i ^ step) for i in range(ndp)]
        temp_part = pl.pallas_call(
            add_kernel,
            out_shape=jax.ShapeDtypeStruct((8, 128), jnp.float32),
            in_specs=[VMEM] * 2,
            out_specs=VMEM,
            compiler_params=params(1),
            name="temp_add",
        )(temp_part, lax.ppermute(temp_part, "dp", pairs))
        step *= 2
    out_send = pl.pallas_call(
        route_kernel,
        out_shape=jax.ShapeDtypeStruct((NCTX, SEND, 256), jnp.bfloat16),
        in_specs=[SMEM, VMEM, VMEM, HBM],
        out_specs=HBM,
        scratch_shapes=[
            pltpu.VMEM((NCTX, CAP * QR + 16, 256), jnp.bfloat16),
            pltpu.SMEM((NCTX,), jnp.int32),
            pltpu.SemaphoreType.DMA((1,)),
        ],
        input_output_aliases={3: 0},
        compiler_params=params(50),
        name="route_dkv",
    )(meta, dkv_recv, temp_part, dq_send)
    out_recv = lax.all_to_all(out_send, "ctx", split_axis=0, concat_axis=0, tiled=True)
    return pl.pallas_call(
        rows_kernel,
        out_shape=(
            jax.ShapeDtypeStruct((1, CAP * BLK, NCTX * 256), jnp.bfloat16),
            jax.ShapeDtypeStruct((1, CAP * BLK, 2 * KV * DH), jnp.bfloat16),
            jax.ShapeDtypeStruct((TEMPS,), jnp.float32),
        ),
        in_specs=[VMEM],
        out_specs=(HBM, VMEM, SMEM),
        scratch_shapes=[
            pltpu.VMEM((CAP * BLK, NCTX * 256), jnp.bfloat16),
            pltpu.SemaphoreType.DMA((2 * CAP,)),
        ],
        compiler_params=params(24),
        name="rows",
    )(out_recv)


def solution(mesh):
    return jax.shard_map(
        shards,
        mesh=mesh,
        in_specs=(
            P("dp", "ctx", None),
            P("dp", "ctx", None),
            P("dp", "ctx", None),
            P("dp", "ctx", None),
            P("dp", None),
            P("dp", None),
            P(),
            P("dp", None, None),
        ),
        out_specs=(P("dp", "ctx", None), P("dp", "ctx", None), P()),
        check_vma=False,
    )
```
